32 devices in a mesh: heads: 2 (over core), tokens: 16 (over z, y, x).
Axes of the slice: x: 2, y: 2, z: 4, core: 2. Of those that a mesh axis runs over, the one named last changes fastest.
Arguments:
- queries: bfloat16 [2, 2048, 2048], P(None, 'tokens', 'heads'), may hold values from -8.5 to 8.5, as said below
- keys: bfloat16 [2, 2048, 2048], P(None, 'tokens', 'heads'), may hold values from -6 to 6
- values: bfloat16 [2, 2048, 2048], P(None, 'tokens', 'heads'), may hold values from -6 to 6
- rates: float32 [2, 8, 2048], P(None, 'heads', 'tokens'), may hold values from 0.05 to 1
- fast_init: bfloat16 [8, 3, 256, 256], P('heads'), may hold values from -0.375 to 0.375
- out_gain: float32 [2048], P('heads'), may hold values from 0.25 to 1.75
Outputs:
- mixed: bfloat16 [2, 2048, 2048], P(None, 'tokens', 'heads')
- final_weights: bfloat16 [8, 3, 256, 256], P('heads')
The draws below stay inside these ranges and needn't reach their ends.
Inputs may be any that keep to these rules, and one draw needn't show every extreme that they name: queries are real-valued and of order one.
All inputs are finite; a program needn't handle non-finite values.
Results may differ from the reference program's by a relative error of at most 0.0095.
Values may be sent and summed in bfloat16 or wider, within the bound.
A program may use at most 64 MiB of HBM per device.

```python
import math
import jax
import jax.numpy as jnp
from jax import lax

HEADS = 8
DH = 256
D = 2048
GROUPS = 2
NS_STEPS = 2
GROUP = 2048


def draw_queries(key, part):
    first = jax.random.fold_in(jax.random.fold_in(key, 11), 0)
    column_head = jnp.arange(D) // DH
    scale = 0.6 + 0.8 * column_head.astype(jnp.float32) / (HEADS - 1)
    base = jnp.clip(jax.random.normal(first, (GROUPS, GROUP, D), jnp.float32), -6.0, 6.0)
    return (base * scale[None, None, :]).astype(jnp.bfloat16)


def steps_of(own_key, dims, cuts, low, high):
    def one(position, shards_of):
        heights = jax.random.uniform(jax.random.fold_in(jax.random.fold_in(own_key, 6), position), (shards_of,), jnp.float32, low / len(cuts), high / len(cuts))
        return jnp.repeat(jnp.exp(heights), dims[position] // shards_of).reshape((-1,) + (1,) * (len(dims) - position - 1))

    loudness = one(*cuts[0])
    for cut in cuts[1:]:
        loudness = loudness * one(*cut)
    return loudness


def bell_draw(stream_key, extent, spread, bound, pieces=(), kind=jnp.bfloat16):
    drawn = spread * jax.random.normal(stream_key, extent, jnp.float32)
    if pieces:
        drawn = drawn * steps_of(stream_key, extent, pieces, -0.22, 0.18)
    return jnp.clip(drawn, -bound, bound).astype(kind)


def setup_inputs(seed: int = 0) -> dict:
    splits = jax.random.split(jax.random.key(seed), 7)
    return {
        "queries": draw_queries(jax.random.fold_in(splits[6], 71), 0),
        "keys": bell_draw(splits[1], (GROUPS, GROUP, D), 1.0, 6.0, ((1, 16), (2, 2))),
        "values": bell_draw(splits[2], (GROUPS, GROUP, D), 1.0, 6.0, ((1, 16), (2, 2))),
        "rates": jnp.clip(jnp.exp(math.log(1.0) - 2.9957323 * jax.random.uniform(splits[3], (GROUPS, HEADS, GROUP), jnp.float32) ** steps_of(splits[3], (GROUPS, HEADS, GROUP), ((1, 2), (2, 16)), -0.2, 0.2)), 0.05, 1.0),
        "fast_init": bell_draw(splits[4], (HEADS, 3, DH, DH), DH ** -0.5, 0.375, ((0, 2),)),
        "out_gain": jnp.clip(1.0 + 0.15 * jax.random.normal(splits[5], (D,), jnp.float32), 0.25, 1.75),
    }


coef_a = 3.4445
coef_b = -4.775
coef_c = 2.0315
step_size = 0.5

def newton(grads):
    squares = lax.optimization_barrier(jnp.sum(grads * grads, axis=(1, 2)))
    current = (grads / (jnp.sqrt(squares)[:, None, None] + 1e-07)).astype(jnp.bfloat16)
    for step in range(NS_STEPS):
        wide = current.astype(jnp.float32)
        gram = jnp.einsum('mij,mkj->mik', wide, wide).astype(jnp.bfloat16)
        gram_wide = gram.astype(jnp.float32)
        square = jnp.einsum('mij,mjk->mik', gram_wide, gram_wide)
        mixer = (coef_b * gram_wide + coef_c * square).astype(jnp.bfloat16)
        current = (coef_a * wide + jnp.einsum('mij,mjk->mik', mixer.astype(jnp.float32), wide)).astype(jnp.bfloat16)
    return current

def head_step(items):
    query, key_rows, value_rows, rate, weight = items
    gate_q = jnp.dot(query, weight[0], preferred_element_type=jnp.float32)
    up_q = jnp.dot(query, weight[1], preferred_element_type=jnp.float32)
    hidden_q = (jax.nn.silu(gate_q) * up_q).astype(jnp.bfloat16)
    output = jnp.dot(hidden_q, weight[2], preferred_element_type=jnp.float32)
    gate_k = jnp.dot(key_rows, weight[0], preferred_element_type=jnp.float32)
    up_k = jnp.dot(key_rows, weight[1], preferred_element_type=jnp.float32)
    sig = jax.nn.sigmoid(gate_k)
    hidden = (gate_k * sig * up_k).astype(jnp.bfloat16)
    scaled = (rate[:, None] * value_rows.astype(jnp.float32)).astype(jnp.bfloat16)
    back = jnp.dot(scaled, weight[2].T, preferred_element_type=jnp.float32)
    grad_gate = (back * up_k * sig * (1.0 + gate_k * (1.0 - sig))).astype(jnp.bfloat16)
    grad_up = (back * gate_k * sig).astype(jnp.bfloat16)
    g_gate = jnp.dot(key_rows.T, grad_gate, preferred_element_type=jnp.float32)
    g_up = jnp.dot(key_rows.T, grad_up, preferred_element_type=jnp.float32)
    g_down = jnp.dot(hidden.T, scaled, preferred_element_type=jnp.float32)
    update = newton(jnp.stack([g_gate, g_up, g_down], axis=0))
    fresh = (weight.astype(jnp.float32) + step_size * update.astype(jnp.float32)).astype(jnp.bfloat16)
    return (output, fresh)

def reference(queries, keys, values, rates, fast_init, out_gain):
    weights = fast_init
    mixed = []
    for block in range(GROUPS):
        query = queries[block].reshape(GROUP, HEADS, DH).transpose(1, 0, 2)
        key_rows = keys[block].reshape(GROUP, HEADS, DH).transpose(1, 0, 2)
        value_rows = values[block].reshape(GROUP, HEADS, DH).transpose(1, 0, 2)
        outputs, weights = lax.map(head_step, (query, key_rows, value_rows, rates[block], weights))
        joined = outputs.transpose(1, 0, 2).reshape(GROUP, D)
        meansq = lax.optimization_barrier(jnp.mean(joined * joined, axis=1, keepdims=True))
        mixed.append((joined / jnp.sqrt(meansq + 1e-06) * out_gain[None, :]).astype(jnp.bfloat16))
    return (jnp.stack(mixed, axis=0), weights)
```

```python
import functools

import jax
import jax.numpy as jnp
from jax import lax
from jax.experimental import pallas as pl
from jax.experimental.pallas import tpu as pltpu
from jax.sharding import PartitionSpec as P

D = 2048
NS_STEPS = 2


coef_a = 3.4445
coef_b = -4.775
coef_c = 2.0315
step_size = 0.5


def newton(current):
    for step in range(NS_STEPS):
        gram = jnp.einsum(
            "hmij,hmkj->hmik", current, current, preferred_element_type=jnp.float32
        ).astype(jnp.bfloat16)
        square = jnp.einsum("hmij,hmjk->hmik", gram, gram, preferred_element_type=jnp.float32)
        mixer = (coef_b * gram.astype(jnp.float32) + coef_c * square).astype(jnp.bfloat16)
        product = jnp.einsum("hmij,hmjk->hmik", mixer, current, preferred_element_type=jnp.float32)
        current = (coef_a * current.astype(jnp.float32) + product).astype(jnp.bfloat16)
    return current


def apply_heads(query, weights):
    gate_q = jnp.einsum("nhd,hde->nhe", query, weights[:, 0], preferred_element_type=jnp.float32)
    up_q = jnp.einsum("nhd,hde->nhe", query, weights[:, 1], preferred_element_type=jnp.float32)
    hidden_q = (jax.nn.silu(gate_q) * up_q).astype(jnp.bfloat16)
    return jnp.einsum("nhd,hde->nhe", hidden_q, weights[:, 2], preferred_element_type=jnp.float32)


def local_grads(key_rows, value_rows, rate, weights):
    gate_k = jnp.einsum("nhd,hde->nhe", key_rows, weights[:, 0], preferred_element_type=jnp.float32)
    up_k = jnp.einsum("nhd,hde->nhe", key_rows, weights[:, 1], preferred_element_type=jnp.float32)
    sig = jax.nn.sigmoid(gate_k)
    hidden = (gate_k * sig * up_k).astype(jnp.bfloat16)
    scaled = (rate.T[:, :, None] * value_rows.astype(jnp.float32)).astype(jnp.bfloat16)
    back = jnp.einsum("nhe,hde->nhd", scaled, weights[:, 2], preferred_element_type=jnp.float32)
    grad_gate = (back * up_k * sig * (1.0 + gate_k * (1.0 - sig))).astype(jnp.bfloat16)
    grad_up = (back * gate_k * sig).astype(jnp.bfloat16)
    g_gate = jnp.einsum("nhd,nhe->hde", key_rows, grad_gate, preferred_element_type=jnp.float32)
    g_up = jnp.einsum("nhd,nhe->hde", key_rows, grad_up, preferred_element_type=jnp.float32)
    g_down = jnp.einsum("nhd,nhe->hde", hidden, scaled, preferred_element_type=jnp.float32)
    return jnp.stack([g_gate, g_up, g_down], axis=1)


def finish(joined, totals, out_gain):
    return (joined / jnp.sqrt(totals[:, None] / D + 1e-06) * out_gain[None, :]).astype(jnp.bfloat16)


def per_device(queries, keys, values, rates, fast_init, out_gain):
    heads_here = fast_init.shape[0]
    head_size = fast_init.shape[2]
    tok_rows = queries.shape[1]
    weights = fast_init
    outputs = []
    joined_all = []
    for block in range(queries.shape[0]):
        query = queries[block].reshape(tok_rows, heads_here, head_size)
        key_rows = keys[block].reshape(tok_rows, heads_here, head_size)
        value_rows = values[block].reshape(tok_rows, heads_here, head_size)
        joined = apply_heads(query, weights).reshape(tok_rows, heads_here * head_size)
        grads = local_grads(key_rows, value_rows, rates[block], weights)
        total = lax.psum(grads, "tokens")
        squares = jnp.sum(total * total, axis=(2, 3))
        start = (total / (jnp.sqrt(squares)[:, :, None, None] + 1e-07)).astype(jnp.bfloat16)
        update = newton(start)
        weights = (weights.astype(jnp.float32) + step_size * update.astype(jnp.float32)).astype(
            jnp.bfloat16
        )
        joined_all.append(joined)
    stacked = jnp.stack(joined_all, axis=0)
    totals = lax.psum(jnp.sum(stacked * stacked, axis=2), "heads")
    outputs = [
        finish(joined_all[index], totals[index], out_gain) for index in range(len(joined_all))
    ]
    return (jnp.stack(outputs, axis=0), weights)


F32 = jnp.float32
BF16 = jnp.bfloat16
MESH = pl.DeviceIdType.MESH
DOWN_FIRST = (2, 0, 1)


def mm(a, b):
    return jnp.dot(a, b, preferred_element_type=F32)


def mm_nt(a, b):
    return lax.dot_general(a, b, (((1,), (1,)), ((), ())), preferred_element_type=F32)


def mm_tn(a, b):
    return lax.dot_general(a, b, (((0,), (0,)), ((), ())), preferred_element_type=F32)


def orthogonalize(mats):
    xs = []
    for g in mats:
        g = g.astype(F32)
        square = jnp.sum(jnp.sum(g * g, axis=1, keepdims=True), axis=0, keepdims=True)
        xs.append((g / (jnp.sqrt(square) + 1e-07)).astype(BF16))
    for _ in range(NS_STEPS):
        grams = [mm_nt(x, x).astype(BF16) for x in xs]
        mixers = [(coef_b * a.astype(F32) + coef_c * mm(a, a)).astype(BF16) for a in grams]
        xs = [(coef_a * x.astype(F32) + mm(b, x)).astype(BF16) for b, x in zip(mixers, xs)]
    return xs


def kernel(
    sizes, q_hbm, k_hbm, v_hbm, r_hbm, w_hbm, gain_ref, mixed_hbm, wout_hbm,
    q0, w0, rates, kv, q1, hid, dp, dg, du, gf, gb, rs, ag, w1, wfull, ysend, ybuf, y0, mix, sq, sqr,
    loc_sem, a2a_s, a2a_r, rs_s, rs_r, ag_s, ag_r, col_s, col_r, fwd_s, fwd_r, y_s, y_r, sq_s, sq_r,
):
    cores, HL, G, rows, DH = sizes
    width = HL * DH
    part = DH // G
    core = lax.axis_index("heads")
    t = lax.axis_index("tokens")
    z = t // G
    p = t % G
    sends = []

    def remote(src, dst, send_sem, recv_sem, device, start=True):
        copy = pltpu.make_async_remote_copy(
            src_ref=src, dst_ref=dst, send_sem=send_sem, recv_sem=recv_sem,
            device_id=device, device_id_type=MESH,
        )
        if start:
            copy.start()
            sends.append(copy)
        return copy

    def head_peer(j):
        return (z + j) % HL

    def plane_peer(j):
        return (p + j) % G

    def at(zz, pp):
        return {"tokens": zz * G + pp}

    def cols(h):
        return pl.ds(pl.multiple_of(h * DH, DH), DH)

    def part_rows(pp):
        return pl.ds(pl.multiple_of(pp * part, part), part)

    local_q = pltpu.make_async_copy(q_hbm.at[0], q0, loc_sem.at[0])
    local_w = pltpu.make_async_copy(w_hbm, w0, loc_sem.at[1])
    local_r = pltpu.make_async_copy(r_hbm, rates.at[z], loc_sem.at[2])
    local_w.start()
    local_q.start()
    local_r.start()
    pieces = [(k_hbm, 0), (v_hbm, 0), (k_hbm, 1), (v_hbm, 1), (q_hbm, 1)]

    def landing(i):
        return q1 if i == 4 else kv.at[i]

    local_pieces = []
    for i, (ref, block) in enumerate(pieces):
        copy = pltpu.make_async_copy(ref.at[block, :, cols(z)], landing(i).at[z], loc_sem.at[3 + i])
        copy.start()
        local_pieces.append(copy)

    barrier = pltpu.get_barrier_semaphore()
    for j in range(1, HL):
        pl.semaphore_signal(barrier, inc=1, device_id=at(head_peer(j), p), device_id_type=MESH)
    for j in range(1, G):
        pl.semaphore_signal(barrier, inc=1, device_id=at(z, plane_peer(j)), device_id_type=MESH)
    for j in range(1, cores):
        pl.semaphore_signal(barrier, inc=1, device_id={"heads": (core + j) % cores}, device_id_type=MESH)
    pl.semaphore_wait(barrier, HL - 1 + G - 1 + cores - 1)

    for j in range(1, HL):
        remote(r_hbm, rates.at[z], a2a_s.at[5, j], a2a_r.at[5, z], at(head_peer(j), p))
    for i, (ref, block) in enumerate(pieces):
        for j in range(1, HL):
            h = head_peer(j)
            remote(ref.at[block, :, cols(h)], landing(i).at[z], a2a_s.at[i, j], a2a_r.at[i, z], at(h, p))

    def arrived(buf, recv_sem, send_sem, device):
        remote(buf, buf, send_sem, recv_sem, device, start=False).wait_recv()

    def piece_arrived(i, j):
        h = head_peer(j)
        if j == 0:
            local_pieces[i].wait()
        else:
            arrived(landing(i).at[h], a2a_r.at[i, h], a2a_s.at[i, j], at(h, p))

    def share_squares(block, square):
        sq[block] = jnp.broadcast_to(square, (rows, 128))
        for j in range(1, cores):
            remote(sq.at[block], sqr.at[block, core], sq_s.at[block, j], sq_r.at[block, core],
                   {"heads": (core + j) % cores})

    def finish_block(block, read):
        total = sq[block]
        for j in range(1, cores):
            other = (core + j) % cores
            arrived(sqr.at[block, other], sq_r.at[block, other], sq_s.at[block, j], {"heads": other})
            total = total + sqr[block, other]
        root = jnp.sqrt(total[:, :1] / (cores * width) + 1e-06)
        for h in range(HL):
            span = slice(h * DH, (h + 1) * DH)
            mix[block, :, span] = (read(h) / root * gain_ref[:, span]).astype(BF16)
        copy = pltpu.make_async_copy(mix.at[block], mixed_hbm.at[block], loc_sem.at[8 + block])
        copy.start()
        return copy

    def fast_net(x, w_gate, w_up, w_down):
        gate = mm(x, w_gate)
        hidden = (jax.nn.silu(gate) * mm(x, w_up)).astype(BF16)
        return mm(hidden, w_down)

    local_w.wait()
    local_q.wait()
    square = jnp.zeros((rows, 1), F32)
    for h in range(HL):
        span = slice(h * DH, (h + 1) * DH)
        y = fast_net(q0[:, span], w0[h, 0], w0[h, 1], w0[h, 2])
        y0[:, span] = y
        square = square + jnp.sum(y * y, axis=1, keepdims=True)
    share_squares(0, square)

    order = [0] + sorted(range(1, HL), key=lambda j: min(j, HL - j))

    def gradients(block, weight):
        for n, j in enumerate(order):
            h = head_peer(j)
            if block == 0:
                if j == 0:
                    local_r.wait()
                else:
                    arrived(rates.at[h], a2a_r.at[5, h], a2a_s.at[5, j], at(h, p))
            piece_arrived(2 * block, j)
            piece_arrived(2 * block + 1, j)
            keys = kv[2 * block, h]
            rate = jnp.broadcast_to(rates[h, block, pl.ds(z, 1), :], (rows, rows)).T[:, :1]
            own = pl.ds(pl.multiple_of(h * rows, rows), rows)
            gate = mm(keys, weight(0))
            up = mm(keys, weight(1))
            sig = jax.nn.sigmoid(gate)
            hid[block, h] = (gate * sig * up).astype(BF16)
            scaled = (rate * kv[2 * block + 1, h].astype(F32)).astype(BF16)
            dp[block, h] = scaled
            back = mm_nt(scaled, weight(2))
            dg[block, h] = (back * up * sig * (1.0 + gate * (1.0 - sig))).astype(BF16)
            du[block, h] = (back * gate * sig).astype(BF16)

        keys = kv[2 * block].reshape(HL * rows, DH)
        pairs = {
            0: lambda: mm_tn(keys, dg[block].reshape(HL * rows, DH)),
            1: lambda: mm_tn(keys, du[block].reshape(HL * rows, DH)),
            2: lambda: mm_tn(hid[block].reshape(HL * rows, DH), dp[block].reshape(HL * rows, DH)),
        }
        for m in DOWN_FIRST:
            grad = pairs[m]()
            gf[block, m] = grad
            gb[block, m] = grad.astype(BF16)
            for j in range(1, G):
                o = plane_peer(j)
                remote(gb.at[block, m, part_rows(o)], rs.at[block, m, p], rs_s.at[block, m, j],
                       rs_r.at[block, m, p], at(z, o))

    def sum_parts(block):
        for m in DOWN_FIRST:
            total = gf[block, m, part_rows(p)]
            for j in range(1, G):
                o = plane_peer(j)
                arrived(rs.at[block, m, o], rs_r.at[block, m, o], rs_s.at[block, m, j], at(z, o))
                total = total + rs[block, m, o].astype(F32)
            ag[block, m, part_rows(p)] = total.astype(BF16)
            for j in range(1, G):
                mine = ag.at[block, m, part_rows(p)]
                remote(mine, mine, ag_s.at[block, m, j], ag_r.at[block, m, p], at(z, plane_peer(j)))

    def summed(block, m):
        for j in range(1, G):
            o = plane_peer(j)
            arrived(ag.at[block, m, part_rows(o)], ag_r.at[block, m, o], ag_s.at[block, m, j], at(z, o))
        return ag[block, m]

    gradients(0, lambda m: w0[z, m])
    out0 = finish_block(0, lambda h: y0[:, h * DH:(h + 1) * DH])
    sum_parts(0)
    updates = orthogonalize([summed(0, m) for m in DOWN_FIRST])
    for m, x in zip(DOWN_FIRST, updates):
        w1[m] = (w0[z, m].astype(F32) + step_size * x.astype(F32)).astype(BF16)

    gradients(1, lambda m: w1[m])
    for j in order:
        h = head_peer(j)
        piece_arrived(4, j)
        y = fast_net(q1[h], w1[0], w1[1], w1[2]).astype(BF16)
        if j == 0:
            ybuf[z] = y
        else:
            ysend[h] = y
            remote(ysend.at[h], ybuf.at[z], y_s.at[j], y_r.at[z], at(h, p))
    sum_parts(1)
    for m in DOWN_FIRST:
        (x,) = orthogonalize([summed(1, m)])
        wfull[z, m] = (w1[m].astype(F32) + step_size * x.astype(F32)).astype(BF16)
        for j in order[1:]:
            mine = wfull.at[z, m, part_rows(p)]
            remote(mine, mine, col_s.at[m, j], col_r.at[m, z], at(head_peer(j), p))
    copies = [out0]
    copy = pltpu.make_async_copy(wfull.at[z], wout_hbm.at[z], loc_sem.at[10])
    copy.start()
    copies.append(copy)

    for j in order[1:]:
        h = head_peer(j)
        arrived(ybuf.at[h], y_r.at[h], y_s.at[j], at(h, p))
    square = jnp.zeros((rows, 1), F32)
    for h in range(HL):
        y = ybuf[h].astype(F32)
        square = square + jnp.sum(y * y, axis=1, keepdims=True)
    share_squares(1, square)

    for j in order[1:]:
        h = head_peer(j)
        for m in DOWN_FIRST:
            mine = wfull.at[h, m, part_rows(p)]
            arrived(mine, col_r.at[m, h], col_s.at[m, j], at(h, p))
            for i in range(1, G):
                remote(mine, mine, fwd_s.at[m, j, i], fwd_r.at[m, h, p], at(z, plane_peer(i)))

    copies.append(finish_block(1, lambda h: ybuf[h].astype(F32)))
    for j in order[1:]:
        h = head_peer(j)
        for m in DOWN_FIRST:
            for i in range(1, G):
                o = plane_peer(i)
                arrived(wfull.at[h, m, part_rows(o)], fwd_r.at[m, h, o], fwd_s.at[m, j, i], at(z, o))
        copy = pltpu.make_async_copy(wfull.at[h], wout_hbm.at[h], loc_sem.at[10 + j])
        copy.start()
        copies.append(copy)
    for copy in sends:
        copy.wait_send()
    for copy in copies:
        copy.wait()


def one_kernel(cores, token_devices, queries, keys, values, rates, fast_init, out_gain):
    blocks, rows, width = queries.shape
    HL, _, DH, _ = fast_init.shape
    G = token_devices // HL
    dma = pltpu.SemaphoreType.DMA
    tokens = (2, HL, rows, DH)
    mats = (2, 3, DH, DH)
    any_space = pl.BlockSpec(memory_space=pl.ANY)
    return pl.pallas_call(
        functools.partial(kernel, (cores, HL, G, rows, DH)),
        out_shape=(
            jax.ShapeDtypeStruct(queries.shape, BF16),
            jax.ShapeDtypeStruct(fast_init.shape, BF16),
        ),
        in_specs=[any_space] * 5 + [pl.BlockSpec(memory_space=pltpu.VMEM)],
        out_specs=(any_space, any_space),
        scratch_shapes=[
            pltpu.VMEM((rows, width), BF16),
            pltpu.VMEM(fast_init.shape, BF16),
            pltpu.VMEM((HL,) + rates.shape, F32),
            pltpu.VMEM((4, HL, rows, DH), BF16),
            pltpu.VMEM((HL, rows, DH), BF16),
            pltpu.VMEM(tokens, BF16),
            pltpu.VMEM(tokens, BF16),
            pltpu.VMEM(tokens, BF16),
            pltpu.VMEM(tokens, BF16),
            pltpu.VMEM(mats, F32),
            pltpu.VMEM(mats, BF16),
            pltpu.VMEM((2, 3, G, DH // G, DH), BF16),
            pltpu.VMEM(mats, BF16),
            pltpu.VMEM((3, DH, DH), BF16),
            pltpu.VMEM(fast_init.shape, BF16),
            pltpu.VMEM((HL, rows, DH), BF16),
            pltpu.VMEM((HL, rows, DH), BF16),
            pltpu.VMEM((rows, width), F32),
            pltpu.VMEM(queries.shape, BF16),
            pltpu.VMEM((2, rows, 128), F32),
            pltpu.VMEM((2, cores, rows, 128), F32),
            dma((10 + HL,)),
            dma((6, HL)), dma((6, HL)),
            dma((2, 3, G)), dma((2, 3, G)),
            dma((2, 3, G)), dma((2, 3, G)),
            dma((3, HL)), dma((3, HL)),
            dma((3, HL, G)), dma((3, HL, G)),
            dma((HL,)), dma((HL,)),
            dma((2, cores)), dma((2, cores)),
        ],
        compiler_params=pltpu.CompilerParams(collective_id=0, has_side_effects=True),
    )(queries, keys, values, rates, fast_init, out_gain.reshape(1, width))


def fits(cores, token_devices, queries, fast_init):
    blocks, rows, width = queries.shape
    HL, _, DH, _ = fast_init.shape
    if blocks != 2 or HL < 2 or token_devices % HL:
        return False
    G = token_devices // HL
    return G > 1 and rows == 128 and DH % (16 * G) == 0 and cores > 1


def per_device_best(cores, token_devices, queries, keys, values, rates, fast_init, out_gain):
    if fits(cores, token_devices, queries, fast_init):
        return one_kernel(cores, token_devices, queries, keys, values, rates, fast_init, out_gain)
    return per_device(queries, keys, values, rates, fast_init, out_gain)


def solution(mesh):
    in_specs = (
        P(None, "tokens", "heads"),
        P(None, "tokens", "heads"),
        P(None, "tokens", "heads"),
        P(None, "heads", "tokens"),
        P("heads", None, None, None),
        P("heads"),
    )
    out_specs = (P(None, "tokens", "heads"), P("heads", None, None, None))
    return jax.shard_map(
        functools.partial(per_device_best, mesh.shape["heads"], mesh.shape["tokens"]), mesh=mesh, in_specs=in_specs, out_specs=out_specs, check_vma=False
    )
```

```python
import functools

import jax
import jax.numpy as jnp
from jax import lax
from jax.experimental import pallas as pl
from jax.experimental.pallas import tpu as pltpu
from jax.sharding import PartitionSpec as P

D = 2048
NS_STEPS = 2


coef_a = 3.4445
coef_b = -4.775
coef_c = 2.0315
step_size = 0.5


def newton(current):
    for step in range(NS_STEPS):
        gram = jnp.einsum(
            "hmij,hmkj->hmik", current, current, preferred_element_type=jnp.float32
        ).astype(jnp.bfloat16)
        square = jnp.einsum("hmij,hmjk->hmik", gram, gram, preferred_element_type=jnp.float32)
        mixer = (coef_b * gram.astype(jnp.float32) + coef_c * square).astype(jnp.bfloat16)
        product = jnp.einsum("hmij,hmjk->hmik", mixer, current, preferred_element_type=jnp.float32)
        current = (coef_a * current.astype(jnp.float32) + product).astype(jnp.bfloat16)
    return current


def apply_heads(query, weights):
    gate_q = jnp.einsum("nhd,hde->nhe", query, weights[:, 0], preferred_element_type=jnp.float32)
    up_q = jnp.einsum("nhd,hde->nhe", query, weights[:, 1], preferred_element_type=jnp.float32)
    hidden_q = (jax.nn.silu(gate_q) * up_q).astype(jnp.bfloat16)
    return jnp.einsum("nhd,hde->nhe", hidden_q, weights[:, 2], preferred_element_type=jnp.float32)


def local_grads(key_rows, value_rows, rate, weights):
    gate_k = jnp.einsum("nhd,hde->nhe", key_rows, weights[:, 0], preferred_element_type=jnp.float32)
    up_k = jnp.einsum("nhd,hde->nhe", key_rows, weights[:, 1], preferred_element_type=jnp.float32)
    sig = jax.nn.sigmoid(gate_k)
    hidden = (gate_k * sig * up_k).astype(jnp.bfloat16)
    scaled = (rate.T[:, :, None] * value_rows.astype(jnp.float32)).astype(jnp.bfloat16)
    back = jnp.einsum("nhe,hde->nhd", scaled, weights[:, 2], preferred_element_type=jnp.float32)
    grad_gate = (back * up_k * sig * (1.0 + gate_k * (1.0 - sig))).astype(jnp.bfloat16)
    grad_up = (back * gate_k * sig).astype(jnp.bfloat16)
    g_gate = jnp.einsum("nhd,nhe->hde", key_rows, grad_gate, preferred_element_type=jnp.float32)
    g_up = jnp.einsum("nhd,nhe->hde", key_rows, grad_up, preferred_element_type=jnp.float32)
    g_down = jnp.einsum("nhd,nhe->hde", hidden, scaled, preferred_element_type=jnp.float32)
    return jnp.stack([g_gate, g_up, g_down], axis=1)


def finish(joined, totals, out_gain):
    return (joined / jnp.sqrt(totals[:, None] / D + 1e-06) * out_gain[None, :]).astype(jnp.bfloat16)


def per_device(queries, keys, values, rates, fast_init, out_gain):
    heads_here = fast_init.shape[0]
    head_size = fast_init.shape[2]
    tok_rows = queries.shape[1]
    weights = fast_init
    outputs = []
    joined_all = []
    for block in range(queries.shape[0]):
        query = queries[block].reshape(tok_rows, heads_here, head_size)
        key_rows = keys[block].reshape(tok_rows, heads_here, head_size)
        value_rows = values[block].reshape(tok_rows, heads_here, head_size)
        joined = apply_heads(query, weights).reshape(tok_rows, heads_here * head_size)
        grads = local_grads(key_rows, value_rows, rates[block], weights)
        total = lax.psum(grads, "tokens")
        squares = jnp.sum(total * total, axis=(2, 3))
        start = (total / (jnp.sqrt(squares)[:, :, None, None] + 1e-07)).astype(jnp.bfloat16)
        update = newton(start)
        weights = (weights.astype(jnp.float32) + step_size * update.astype(jnp.float32)).astype(
            jnp.bfloat16
        )
        joined_all.append(joined)
    stacked = jnp.stack(joined_all, axis=0)
    totals = lax.psum(jnp.sum(stacked * stacked, axis=2), "heads")
    outputs = [
        finish(joined_all[index], totals[index], out_gain) for index in range(len(joined_all))
    ]
    return (jnp.stack(outputs, axis=0), weights)


F32 = jnp.float32
BF16 = jnp.bfloat16
MESH = pl.DeviceIdType.MESH
DOWN_FIRST = (2, 0, 1)


def mm(a, b):
    return jnp.dot(a, b, preferred_element_type=F32)


def mm_nt(a, b):
    return lax.dot_general(a, b, (((1,), (1,)), ((), ())), preferred_element_type=F32)


def mm_tn(a, b):
    return lax.dot_general(a, b, (((0,), (0,)), ((), ())), preferred_element_type=F32)


def orthogonalize(mats):
    xs = []
    for g in mats:
        g = g.astype(F32)
        square = jnp.sum(jnp.sum(g * g, axis=1, keepdims=True), axis=0, keepdims=True)
        xs.append((g / (jnp.sqrt(square) + 1e-07)).astype(BF16))
    for _ in range(NS_STEPS):
        grams = [mm_nt(x, x).astype(BF16) for x in xs]
        mixers = [(coef_b * a.astype(F32) + coef_c * mm(a, a)).astype(BF16) for a in grams]
        xs = [(coef_a * x.astype(F32) + mm(b, x)).astype(BF16) for b, x in zip(mixers, xs)]
    return xs


def kernel(
    sizes, q_hbm, k_hbm, v_hbm, r_hbm, w_hbm, gain_hbm, mixed, wout,
    q0, w0, rates, gain, kv, q1, hid, dp, dg, du, gf, gb, rs, ag, w1, ysend, ybuf, y0, sq, sqr,
    loc_sem, a2a_s, kv_r, one_r, rs_s, rs_r, ag_s, ag_r, col_s, col_r, fwd_s, fwd_r, y_s, sq_s, sq_r,
):
    cores, HL, G, rows, DH = sizes
    width = HL * DH
    part = DH // G
    core = lax.axis_index("heads")
    t = lax.axis_index("tokens")
    z = t // G
    p = t % G
    xn = p + 1 - 2 * (p % 2)
    yn = (p + 2) % G
    across = (xn + 2) % G

    def remote(src, dst, send_sem, recv_sem, device):
        return pltpu.make_async_remote_copy(
            src_ref=src, dst_ref=dst, send_sem=send_sem, recv_sem=recv_sem,
            device_id=device, device_id_type=MESH,
        )

    def send(src, dst, send_sem, recv_sem, device):
        remote(src, dst, send_sem, recv_sem, device).start()

    def head_peer(j):
        return (z + j) % HL

    def head_source(j):
        return (z + HL - j) % HL

    def plane_peer(j):
        return (p + j) % G

    def at(zz, pp):
        return {"tokens": zz * G + pp}

    def arrived(ref, recv_sem):
        remote(ref, ref, loc_sem.at[0], recv_sem, at(z, xn)).wait_recv()

    def drained(ref, send_sem):
        remote(ref, ref, send_sem, loc_sem.at[0], at(z, xn)).wait_send()

    def cols(h):
        return pl.ds(pl.multiple_of(h * DH, DH), DH)

    def part_rows(pp):
        return pl.ds(pl.multiple_of(pp * part, part), part)

    local_q = pltpu.make_async_copy(q_hbm.at[0], q0, loc_sem.at[0])
    local_w = pltpu.make_async_copy(w_hbm, w0, loc_sem.at[1])
    local_r = pltpu.make_async_copy(r_hbm, rates.at[z], loc_sem.at[2])
    local_gain = pltpu.make_async_copy(gain_hbm, gain, loc_sem.at[3])
    local_w.start()
    local_q.start()
    local_r.start()
    local_gain.start()
    pieces = [(k_hbm, 0), (v_hbm, 0), (k_hbm, 1), (v_hbm, 1), (q_hbm, 1)]

    def landing(i):
        return q1 if i == 4 else kv.at[i]

    local_pieces = []
    for i, (ref, block) in enumerate(pieces):
        copy = pltpu.make_async_copy(ref.at[block, :, cols(z)], landing(i).at[z], loc_sem.at[4 + i])
        copy.start()
        local_pieces.append(copy)

    barrier = pltpu.get_barrier_semaphore()
    for j in range(1, HL):
        pl.semaphore_signal(barrier, inc=1, device_id=at(head_peer(j), p), device_id_type=MESH)
    for j in range(1, G):
        pl.semaphore_signal(barrier, inc=1, device_id=at(z, plane_peer(j)), device_id_type=MESH)
    for j in range(1, cores):
        pl.semaphore_signal(barrier, inc=1, device_id={"heads": (core + j) % cores}, device_id_type=MESH)
    pl.semaphore_wait(barrier, HL - 1 + G - 1 + cores - 1)

    for j in range(1, HL):
        send(r_hbm, rates.at[z], a2a_s.at[5], one_r.at[0], at(head_peer(j), p))
    for i, (ref, block) in enumerate(pieces):
        for j in range(1, HL):
            h = head_peer(j)
            recv = one_r.at[1] if i == 4 else kv_r.at[block, j - 1]
            send(ref.at[block, :, cols(h)], landing(i).at[z], a2a_s.at[i], recv, at(h, p))

    def share_squares(block, square):
        sq[block] = jnp.broadcast_to(square, (rows, 128))
        for j in range(1, cores):
            send(sq.at[block], sqr.at[block, j - 1], sq_s.at[block], sq_r.at[block],
                 {"heads": (core + j) % cores})

    def finish_block(block, read):
        total = sq[block]
        arrived(sqr.at[block], sq_r.at[block])
        for j in range(1, cores):
            total = total + sqr[block, j - 1]
        root = jnp.sqrt(total[:, :1] / (cores * width) + 1e-06)
        for h in range(HL):
            span = slice(h * DH, (h + 1) * DH)
            mixed[block, :, span] = (read(h) / root * gain[:, span]).astype(BF16)

    def fast_net(x, w_gate, w_up, w_down):
        gate = mm(x, w_gate)
        hidden = (jax.nn.silu(gate) * mm(x, w_up)).astype(BF16)
        return mm(hidden, w_down)

    def share(view, send_sem, recv_x, recv_y, recv_r):
        mine = view(part_rows(p))
        send(mine, mine, send_sem, recv_x, at(z, xn))
        send(mine, mine, send_sem, recv_y, at(z, yn))
        send(mine, mine, send_sem, recv_r, at(z, across))

    def shared(view, recv_x, recv_y):
        arrived(view(part_rows(xn)), recv_x)
        arrived(view(part_rows(yn)), recv_y)

    local_w.wait()
    local_q.wait()
    square = jnp.zeros((rows, 1), F32)
    for h in range(HL):
        span = slice(h * DH, (h + 1) * DH)
        y = fast_net(q0[:, span], w0[h, 0], w0[h, 1], w0[h, 2])
        y0[:, span] = y
        square = square + jnp.sum(y * y, axis=1, keepdims=True)
    share_squares(0, square)

    order = [0] + sorted(range(1, HL), key=lambda j: min(j, HL - j))

    def gradients(block, weight):
        for j in order:
            h = head_source(j)
            if j == 0:
                local_pieces[2 * block].wait()
                local_pieces[2 * block + 1].wait()
                if block == 0:
                    local_r.wait()
                    arrived(rates.at[pl.ds(0, HL - 1)], one_r.at[0])
            else:
                arrived(kv.at[pl.ds(2 * block, 2), h], kv_r.at[block, j - 1])
            keys = kv[2 * block, h]
            rate = jnp.broadcast_to(rates[h, block, pl.ds(z, 1), :], (rows, rows)).T[:, :1]
            gate = mm(keys, weight(0))
            up = mm(keys, weight(1))
            sig = jax.nn.sigmoid(gate)
            hid[block, h] = (gate * sig * up).astype(BF16)
            scaled = (rate * kv[2 * block + 1, h].astype(F32)).astype(BF16)
            dp[block, h] = scaled
            back = mm_nt(scaled, weight(2))
            dg[block, h] = (back * up * sig * (1.0 + gate * (1.0 - sig))).astype(BF16)
            du[block, h] = (back * gate * sig).astype(BF16)
        keys = kv[2 * block].reshape(HL * rows, DH)
        pairs = {
            0: lambda: mm_tn(keys, dg[block].reshape(HL * rows, DH)),
            1: lambda: mm_tn(keys, du[block].reshape(HL * rows, DH)),
            2: lambda: mm_tn(hid[block].reshape(HL * rows, DH), dp[block].reshape(HL * rows, DH)),
        }
        for m in DOWN_FIRST:
            grad = pairs[m]()
            gf[block, m] = grad
            gb[block, m] = grad.astype(BF16)
            for j in range(1, G):
                o = plane_peer(j)
                send(gb.at[block, m, part_rows(o)], rs.at[block, m, j - 1], rs_s.at[block],
                     rs_r.at[block, m], at(z, o))

    def ag_view(block, m):
        return lambda span: ag.at[block, m, span]

    def sum_parts(block):
        for m in DOWN_FIRST:
            total = gf[block, m, part_rows(p)]
            arrived(rs.at[block, m], rs_r.at[block, m])
            for j in range(1, G):
                total = total + rs[block, m, j - 1].astype(F32)
            ag[block, m, part_rows(p)] = total.astype(BF16)
            share(ag_view(block, m), ag_s.at[block], ag_r.at[block, m, 0], ag_r.at[block, m, 1], ag_r.at[block, m, 2])
        for m in DOWN_FIRST:
            shared(ag_view(block, m), ag_r.at[block, m, 0], ag_r.at[block, m, 1])

    def summed(block, m):
        arrived(ag.at[block, m, part_rows(across)], ag_r.at[block, m, 2])
        return ag[block, m]

    gradients(0, lambda m: w0[z, m])
    local_gain.wait()
    finish_block(0, lambda h: y0[:, h * DH:(h + 1) * DH])
    sum_parts(0)
    updates = orthogonalize([summed(0, m) for m in DOWN_FIRST])
    for m, x in zip(DOWN_FIRST, updates):
        w1[m] = (w0[z, m].astype(F32) + step_size * x.astype(F32)).astype(BF16)

    gradients(1, lambda m: w1[m])
    local_pieces[4].wait()
    arrived(q1.at[pl.ds(0, HL - 1)], one_r.at[1])
    for j in order:
        h = head_peer(j)
        y = fast_net(q1[h], w1[0], w1[1], w1[2]).astype(BF16)
        if j == 0:
            ybuf[z] = y
        else:
            ysend[h] = y
            send(ysend.at[h], ybuf.at[z], y_s.at[0], one_r.at[2], at(h, p))
    sum_parts(1)
    for m in DOWN_FIRST:
        (x,) = orthogonalize([summed(1, m)])
        wout[z, m] = (w1[m].astype(F32) + step_size * x.astype(F32)).astype(BF16)
        for j in order[1:]:
            mine = wout.at[z, m, part_rows(p)]
            send(mine, mine, col_s.at[0], col_r.at[m, j - 1], at(head_peer(j), p))

    arrived(ybuf.at[pl.ds(0, HL - 1)], one_r.at[2])
    square = jnp.zeros((rows, 1), F32)
    for h in range(HL):
        y = ybuf[h].astype(F32)
        square = square + jnp.sum(y * y, axis=1, keepdims=True)
    share_squares(1, square)

    def wout_view(m, j):
        return lambda span: wout.at[head_source(j), m, span]

    items = [(m, j) for m in DOWN_FIRST for j in order[1:]]
    for m, j in items:
        arrived(wout_view(m, j)(part_rows(p)), col_r.at[m, j - 1])
        share(wout_view(m, j), fwd_s.at[0], fwd_r.at[0, m, j - 1], fwd_r.at[1, m, j - 1], one_r.at[3])
    for m, j in items:
        shared(wout_view(m, j), fwd_r.at[0, m, j - 1], fwd_r.at[1, m, j - 1])
    finish_block(1, lambda h: ybuf[h].astype(F32))
    arrived(wout.at[pl.ds(0, HL - 1), :, pl.ds(0, part)], one_r.at[3])

    for i in range(5):
        drained(q1.at[pl.ds(0, HL - 1)], a2a_s.at[i])
    drained(rates.at[pl.ds(0, HL - 1)], a2a_s.at[5])
    for block in range(2):
        drained(rs.at[block], rs_s.at[block])
        drained(rs.at[block], ag_s.at[block])
        drained(sqr.at[block], sq_s.at[block])
    drained(wout.at[pl.ds(0, HL - 1), :, pl.ds(0, part)], col_s.at[0])
    drained(wout.at[pl.ds(0, HL - 1), :, pl.ds(0, 3 * part)], fwd_s.at[0])
    drained(ysend.at[pl.ds(0, HL - 1)], y_s.at[0])


def one_kernel(cores, token_devices, queries, keys, values, rates, fast_init, out_gain):
    blocks, rows, width = queries.shape
    HL, _, DH, _ = fast_init.shape
    G = token_devices // HL
    dma = lambda *shape: pltpu.SemaphoreType.DMA(shape)
    tokens = (2, HL, rows, DH)
    mats = (2, 3, DH, DH)
    any_space = pl.BlockSpec(memory_space=pl.ANY)
    in_vmem = pl.BlockSpec(memory_space=pltpu.VMEM)
    return pl.pallas_call(
        functools.partial(kernel, (cores, HL, G, rows, DH)),
        out_shape=(pltpu.VMEM(queries.shape, BF16), pltpu.VMEM(fast_init.shape, BF16)),
        in_specs=[any_space] * 6,
        out_specs=(in_vmem, in_vmem),
        scratch_shapes=[
            pltpu.VMEM((rows, width), BF16),
            pltpu.VMEM(fast_init.shape, BF16),
            pltpu.VMEM((HL,) + rates.shape, F32),
            pltpu.VMEM((1, width), F32),
            pltpu.VMEM((4, HL, rows, DH), BF16),
            pltpu.VMEM((HL, rows, DH), BF16),
            pltpu.VMEM(tokens, BF16),
            pltpu.VMEM(tokens, BF16),
            pltpu.VMEM(tokens, BF16),
            pltpu.VMEM(tokens, BF16),
            pltpu.VMEM(mats, F32),
            pltpu.VMEM(mats, BF16),
            pltpu.VMEM((2, 3, G - 1, DH // G, DH), BF16),
            pltpu.VMEM(mats, BF16),
            pltpu.VMEM((3, DH, DH), BF16),
            pltpu.VMEM((HL, rows, DH), BF16),
            pltpu.VMEM((HL, rows, DH), BF16),
            pltpu.VMEM((rows, width), F32),
            pltpu.VMEM((2, rows, 128), F32),
            pltpu.VMEM((2, cores - 1, rows, 128), F32),
            dma(9),
            dma(6), dma(2, HL - 1), dma(4),
            dma(2), dma(2, 3),
            dma(2), dma(2, 3, 3),
            dma(1), dma(3, HL - 1),
            dma(1), dma(2, 3, HL - 1),
            dma(1), dma(2), dma(2),
        ],
        compiler_params=pltpu.CompilerParams(collective_id=0, has_side_effects=True),
    )(queries, keys, values, rates, fast_init, out_gain.reshape(1, width))


def fits(cores, token_devices, queries, fast_init):
    blocks, rows, width = queries.shape
    HL, _, DH, _ = fast_init.shape
    return (
        blocks == 2 and HL > 1 and cores > 1 and token_devices == 4 * HL
        and rows == 128 and DH % 128 == 0
    )


def per_device_best(cores, token_devices, queries, keys, values, rates, fast_init, out_gain):
    if fits(cores, token_devices, queries, fast_init):
        return one_kernel(cores, token_devices, queries, keys, values, rates, fast_init, out_gain)
    return per_device(queries, keys, values, rates, fast_init, out_gain)


def solution(mesh):
    in_specs = (
        P(None, "tokens", "heads"),
        P(None, "tokens", "heads"),
        P(None, "tokens", "heads"),
        P(None, "heads", "tokens"),
        P("heads", None, None, None),
        P("heads"),
    )
    out_specs = (P(None, "tokens", "heads"), P("heads", None, None, None))
    return jax.shard_map(
        functools.partial(per_device_best, mesh.shape["heads"], mesh.shape["tokens"]), mesh=mesh, in_specs=in_specs, out_specs=out_specs, check_vma=False
    )
```

```python
import functools

import jax
import jax.numpy as jnp
from jax import lax
from jax.experimental import pallas as pl
from jax.experimental.pallas import tpu as pltpu
from jax.sharding import PartitionSpec as P

D = 2048
NS_STEPS = 2


coef_a = 3.4445
coef_b = -4.775
coef_c = 2.0315
step_size = 0.5


def newton(current):
    for step in range(NS_STEPS):
        gram = jnp.einsum(
            "hmij,hmkj->hmik", current, current, preferred_element_type=jnp.float32
        ).astype(jnp.bfloat16)
        square = jnp.einsum("hmij,hmjk->hmik", gram, gram, preferred_element_type=jnp.float32)
        mixer = (coef_b * gram.astype(jnp.float32) + coef_c * square).astype(jnp.bfloat16)
        product = jnp.einsum("hmij,hmjk->hmik", mixer, current, preferred_element_type=jnp.float32)
        current = (coef_a * current.astype(jnp.float32) + product).astype(jnp.bfloat16)
    return current


def apply_heads(query, weights):
    gate_q = jnp.einsum("nhd,hde->nhe", query, weights[:, 0], preferred_element_type=jnp.float32)
    up_q = jnp.einsum("nhd,hde->nhe", query, weights[:, 1], preferred_element_type=jnp.float32)
    hidden_q = (jax.nn.silu(gate_q) * up_q).astype(jnp.bfloat16)
    return jnp.einsum("nhd,hde->nhe", hidden_q, weights[:, 2], preferred_element_type=jnp.float32)


def local_grads(key_rows, value_rows, rate, weights):
    gate_k = jnp.einsum("nhd,hde->nhe", key_rows, weights[:, 0], preferred_element_type=jnp.float32)
    up_k = jnp.einsum("nhd,hde->nhe", key_rows, weights[:, 1], preferred_element_type=jnp.float32)
    sig = jax.nn.sigmoid(gate_k)
    hidden = (gate_k * sig * up_k).astype(jnp.bfloat16)
    scaled = (rate.T[:, :, None] * value_rows.astype(jnp.float32)).astype(jnp.bfloat16)
    back = jnp.einsum("nhe,hde->nhd", scaled, weights[:, 2], preferred_element_type=jnp.float32)
    grad_gate = (back * up_k * sig * (1.0 + gate_k * (1.0 - sig))).astype(jnp.bfloat16)
    grad_up = (back * gate_k * sig).astype(jnp.bfloat16)
    g_gate = jnp.einsum("nhd,nhe->hde", key_rows, grad_gate, preferred_element_type=jnp.float32)
    g_up = jnp.einsum("nhd,nhe->hde", key_rows, grad_up, preferred_element_type=jnp.float32)
    g_down = jnp.einsum("nhd,nhe->hde", hidden, scaled, preferred_element_type=jnp.float32)
    return jnp.stack([g_gate, g_up, g_down], axis=1)


def finish(joined, totals, out_gain):
    return (joined / jnp.sqrt(totals[:, None] / D + 1e-06) * out_gain[None, :]).astype(jnp.bfloat16)


def per_device(queries, keys, values, rates, fast_init, out_gain):
    heads_here = fast_init.shape[0]
    head_size = fast_init.shape[2]
    tok_rows = queries.shape[1]
    weights = fast_init
    outputs = []
    joined_all = []
    for block in range(queries.shape[0]):
        query = queries[block].reshape(tok_rows, heads_here, head_size)
        key_rows = keys[block].reshape(tok_rows, heads_here, head_size)
        value_rows = values[block].reshape(tok_rows, heads_here, head_size)
        joined = apply_heads(query, weights).reshape(tok_rows, heads_here * head_size)
        grads = local_grads(key_rows, value_rows, rates[block], weights)
        total = lax.psum(grads, "tokens")
        squares = jnp.sum(total * total, axis=(2, 3))
        start = (total / (jnp.sqrt(squares)[:, :, None, None] + 1e-07)).astype(jnp.bfloat16)
        update = newton(start)
        weights = (weights.astype(jnp.float32) + step_size * update.astype(jnp.float32)).astype(
            jnp.bfloat16
        )
        joined_all.append(joined)
    stacked = jnp.stack(joined_all, axis=0)
    totals = lax.psum(jnp.sum(stacked * stacked, axis=2), "heads")
    outputs = [
        finish(joined_all[index], totals[index], out_gain) for index in range(len(joined_all))
    ]
    return (jnp.stack(outputs, axis=0), weights)


F32 = jnp.float32
BF16 = jnp.bfloat16
MESH = pl.DeviceIdType.MESH
DOWN_FIRST = (2, 0, 1)


def mm(a, b):
    return jnp.dot(a, b, preferred_element_type=F32)


def mm_nt(a, b):
    return lax.dot_general(a, b, (((1,), (1,)), ((), ())), preferred_element_type=F32)


def mm_tn(a, b):
    return lax.dot_general(a, b, (((0,), (0,)), ((), ())), preferred_element_type=F32)


def orthogonalize(mats):
    xs = []
    for g in mats:
        g = g.astype(F32)
        square = jnp.sum(jnp.sum(g * g, axis=1, keepdims=True), axis=0, keepdims=True)
        xs.append((g / (jnp.sqrt(square) + 1e-07)).astype(BF16))
    for _ in range(NS_STEPS):
        grams = [mm_nt(x, x).astype(BF16) for x in xs]
        mixers = [(coef_b * a.astype(F32) + coef_c * mm(a, a)).astype(BF16) for a in grams]
        xs = [(coef_a * x.astype(F32) + mm(b, x)).astype(BF16) for b, x in zip(mixers, xs)]
    return xs


def kernel(
    sizes, q_hbm, k_hbm, v_hbm, r_hbm, w_hbm, gain_hbm, mixed, wout,
    q0, w0, rates, gain, kv, q1, hid, dp, dg, du, gf, gb, rs, ag, w1, ysend, ybuf, y0, sq, sqr,
    loc_sem, a2a_s, kv_r, one_r, rs_s, rs_r, ag_s, ag_r, col_s, col_r, fwd_s, fwd_r, y_s, sq_s, sq_r,
):
    cores, HL, G, rows, DH = sizes
    width = HL * DH
    part = DH // G
    half = part // 2
    core = lax.axis_index("heads")
    t = lax.axis_index("tokens")
    z = t // G
    p = t % G
    xn = p + 1 - 2 * (p % 2)
    yn = (p + 2) % G
    across = (xn + 2) % G

    def remote(src, dst, send_sem, recv_sem, device):
        return pltpu.make_async_remote_copy(
            src_ref=src, dst_ref=dst, send_sem=send_sem, recv_sem=recv_sem,
            device_id=device, device_id_type=MESH,
        )

    def send(src, dst, send_sem, recv_sem, device):
        remote(src, dst, send_sem, recv_sem, device).start()

    def head_peer(j):
        return (z + j) % HL

    def head_source(j):
        return (z + HL - j) % HL

    def plane_peer(j):
        return (p + j) % G

    def at(zz, pp):
        return {"tokens": zz * G + pp}

    def arrived(ref, recv_sem):
        remote(ref, ref, loc_sem.at[0], recv_sem, at(z, xn)).wait_recv()

    def drained(ref, send_sem):
        remote(ref, ref, send_sem, loc_sem.at[0], at(z, xn)).wait_send()

    def cols(h):
        return pl.ds(pl.multiple_of(h * DH, DH), DH)

    def part_rows(pp):
        return pl.ds(pl.multiple_of(pp * part, part), part)

    def half_rows(pp, which):
        return pl.ds(pl.multiple_of(pp * part + which * half, half), half)

    local_q = pltpu.make_async_copy(q_hbm.at[0], q0, loc_sem.at[0])
    local_w = pltpu.make_async_copy(w_hbm, w0, loc_sem.at[1])
    local_r = pltpu.make_async_copy(r_hbm, rates.at[z], loc_sem.at[2])
    local_gain = pltpu.make_async_copy(gain_hbm, gain, loc_sem.at[3])
    local_w.start()
    local_q.start()
    local_r.start()
    local_gain.start()
    pieces = [(k_hbm, 0), (v_hbm, 0), (k_hbm, 1), (v_hbm, 1), (q_hbm, 1)]

    def landing(i):
        return q1 if i == 4 else kv.at[i]

    local_pieces = []
    for i, (ref, block) in enumerate(pieces):
        copy = pltpu.make_async_copy(ref.at[block, :, cols(z)], landing(i).at[z], loc_sem.at[4 + i])
        copy.start()
        local_pieces.append(copy)

    barrier = pltpu.get_barrier_semaphore()
    for j in range(1, HL):
        pl.semaphore_signal(barrier, inc=1, device_id=at(head_peer(j), p), device_id_type=MESH)
    for j in range(1, G):
        pl.semaphore_signal(barrier, inc=1, device_id=at(z, plane_peer(j)), device_id_type=MESH)
    for j in range(1, cores):
        pl.semaphore_signal(barrier, inc=1, device_id={"heads": (core + j) % cores}, device_id_type=MESH)
    pl.semaphore_wait(barrier, HL - 1 + G - 1 + cores - 1)

    for j in range(1, HL):
        send(r_hbm, rates.at[z], a2a_s.at[5], one_r.at[0], at(head_peer(j), p))
    for i, (ref, block) in enumerate(pieces):
        for j in range(1, HL):
            h = head_peer(j)
            recv = one_r.at[1] if i == 4 else kv_r.at[block, j - 1]
            send(ref.at[block, :, cols(h)], landing(i).at[z], a2a_s.at[i], recv, at(h, p))

    def share_squares(block, square):
        sq[block] = jnp.broadcast_to(square, (rows, 128))
        for j in range(1, cores):
            send(sq.at[block], sqr.at[block, j - 1], sq_s.at[block], sq_r.at[block],
                 {"heads": (core + j) % cores})

    def finish_block(block, read):
        total = sq[block]
        arrived(sqr.at[block], sq_r.at[block])
        for j in range(1, cores):
            total = total + sqr[block, j - 1]
        root = jnp.sqrt(total[:, :1] / (cores * width) + 1e-06)
        for h in range(HL):
            span = slice(h * DH, (h + 1) * DH)
            mixed[block, :, span] = (read(h) / root * gain[:, span]).astype(BF16)

    def fast_net(x, w_gate, w_up, w_down):
        gate = mm(x, w_gate)
        hidden = (jax.nn.silu(gate) * mm(x, w_up)).astype(BF16)
        return mm(hidden, w_down)

    def share(view, send_sem, recv_x, recv_y, recv_r):
        mine = view(part_rows(p))
        send(mine, mine, send_sem, recv_x, at(z, xn))
        send(mine, mine, send_sem, recv_y, at(z, yn))
        send(mine, mine, send_sem, recv_r, at(z, across))

    def shared(view, recv_x, recv_y):
        arrived(view(part_rows(xn)), recv_x)
        arrived(view(part_rows(yn)), recv_y)

    def pass_on(view, send_sem, recv_x, recv_y, recv_relay):
        arrived(view(part_rows(xn)), recv_x)
        first = view(half_rows(xn, 0))
        send(first, first, send_sem, recv_relay, at(z, yn))
        arrived(view(part_rows(yn)), recv_y)
        second = view(half_rows(yn, 1))
        send(second, second, send_sem, recv_relay, at(z, xn))

    local_w.wait()
    local_q.wait()
    square = jnp.zeros((rows, 1), F32)
    for h in range(HL):
        span = slice(h * DH, (h + 1) * DH)
        y = fast_net(q0[:, span], w0[h, 0], w0[h, 1], w0[h, 2])
        y0[:, span] = y
        square = square + jnp.sum(y * y, axis=1, keepdims=True)
    share_squares(0, square)

    order = [0] + sorted(range(1, HL), key=lambda j: min(j, HL - j))

    def gradients(block, weight):
        for j in order:
            h = head_source(j)
            if j == 0:
                local_pieces[2 * block].wait()
                local_pieces[2 * block + 1].wait()
                if block == 0:
                    local_r.wait()
                    arrived(rates.at[pl.ds(0, HL - 1)], one_r.at[0])
            else:
                arrived(kv.at[pl.ds(2 * block, 2), h], kv_r.at[block, j - 1])
            keys = kv[2 * block, h]
            rate = jnp.broadcast_to(rates[h, block, pl.ds(z, 1), :], (rows, rows)).T[:, :1]
            gate = mm(keys, weight(0))
            up = mm(keys, weight(1))
            sig = jax.nn.sigmoid(gate)
            hid[block, h] = (gate * sig * up).astype(BF16)
            scaled = (rate * kv[2 * block + 1, h].astype(F32)).astype(BF16)
            dp[block, h] = scaled
            back = mm_nt(scaled, weight(2))
            dg[block, h] = (back * up * sig * (1.0 + gate * (1.0 - sig))).astype(BF16)
            du[block, h] = (back * gate * sig).astype(BF16)
        keys = kv[2 * block].reshape(HL * rows, DH)
        pairs = {
            0: lambda: mm_tn(keys, dg[block].reshape(HL * rows, DH)),
            1: lambda: mm_tn(keys, du[block].reshape(HL * rows, DH)),
            2: lambda: mm_tn(hid[block].reshape(HL * rows, DH), dp[block].reshape(HL * rows, DH)),
        }
        for m in DOWN_FIRST:
            grad = pairs[m]()
            gf[block, m] = grad
            gb[block, m] = grad.astype(BF16)
            for j in range(1, G):
                o = plane_peer(j)
                send(gb.at[block, m, part_rows(o)], rs.at[block, m, j - 1], rs_s.at[block],
                     rs_r.at[block, m], at(z, o))

    def ag_view(block, m):
        return lambda span: ag.at[block, m, span]

    def sum_parts(block):
        for m in DOWN_FIRST:
            total = gf[block, m, part_rows(p)]
            arrived(rs.at[block, m], rs_r.at[block, m])
            for j in range(1, G):
                total = total + rs[block, m, j - 1].astype(F32)
            ag[block, m, part_rows(p)] = total.astype(BF16)
            share(ag_view(block, m), ag_s.at[block], ag_r.at[block, m, 0], ag_r.at[block, m, 1], ag_r.at[block, m, 2])
        for m in DOWN_FIRST:
            shared(ag_view(block, m), ag_r.at[block, m, 0], ag_r.at[block, m, 1])

    def summed(block, m):
        arrived(ag.at[block, m, part_rows(across)], ag_r.at[block, m, 2])
        return ag[block, m]

    gradients(0, lambda m: w0[z, m])
    local_gain.wait()
    finish_block(0, lambda h: y0[:, h * DH:(h + 1) * DH])
    sum_parts(0)
    updates = orthogonalize([summed(0, m) for m in DOWN_FIRST])
    for m, x in zip(DOWN_FIRST, updates):
        w1[m] = (w0[z, m].astype(F32) + step_size * x.astype(F32)).astype(BF16)

    gradients(1, lambda m: w1[m])
    local_pieces[4].wait()
    arrived(q1.at[pl.ds(0, HL - 1)], one_r.at[1])
    for j in order:
        h = head_peer(j)
        y = fast_net(q1[h], w1[0], w1[1], w1[2]).astype(BF16)
        if j == 0:
            ybuf[z] = y
        else:
            ysend[h] = y
            send(ysend.at[h], ybuf.at[z], y_s.at[0], one_r.at[2], at(h, p))
    sum_parts(1)
    for m in DOWN_FIRST:
        (x,) = orthogonalize([summed(1, m)])
        wout[z, m] = (w1[m].astype(F32) + step_size * x.astype(F32)).astype(BF16)
        for j in order[1:]:
            mine = wout.at[z, m, part_rows(p)]
            send(mine, mine, col_s.at[0], col_r.at[m, j - 1], at(head_peer(j), p))

    arrived(ybuf.at[pl.ds(0, HL - 1)], one_r.at[2])
    square = jnp.zeros((rows, 1), F32)
    for h in range(HL):
        y = ybuf[h].astype(F32)
        square = square + jnp.sum(y * y, axis=1, keepdims=True)
    share_squares(1, square)

    def wout_view(m, j):
        return lambda span: wout.at[head_source(j), m, span]

    items = [(m, j) for m in DOWN_FIRST for j in order[1:]]
    passed = len(items) - 3
    for n in range(len(items) + 5):
        if n < len(items):
            m, j = items[n]
            recvs = (fwd_r.at[0, m, j - 1], fwd_r.at[1, m, j - 1])
            arrived(wout_view(m, j)(part_rows(p)), col_r.at[m, j - 1])
            if n < passed:
                mine = wout_view(m, j)(part_rows(p))
                send(mine, mine, fwd_s.at[0], recvs[0], at(z, xn))
                send(mine, mine, fwd_s.at[0], recvs[1], at(z, yn))
            else:
                share(wout_view(m, j), fwd_s.at[0], *recvs, one_r.at[3])
        if n >= 5:
            m, j = items[n - 5]
            recvs = (fwd_r.at[0, m, j - 1], fwd_r.at[1, m, j - 1])
            if n - 5 < passed:
                pass_on(wout_view(m, j), fwd_s.at[0], *recvs, one_r.at[3])
            else:
                shared(wout_view(m, j), *recvs)
    finish_block(1, lambda h: ybuf[h].astype(F32))
    arrived(wout.at[pl.ds(0, HL - 1), :, pl.ds(0, part)], one_r.at[3])

    for i in range(5):
        drained(q1.at[pl.ds(0, HL - 1)], a2a_s.at[i])
    drained(rates.at[pl.ds(0, HL - 1)], a2a_s.at[5])
    for block in range(2):
        drained(rs.at[block], rs_s.at[block])
        drained(rs.at[block], ag_s.at[block])
        drained(sqr.at[block], sq_s.at[block])
    drained(wout.at[pl.ds(0, HL - 1), :, pl.ds(0, part)], col_s.at[0])
    drained(wout.at[pl.ds(0, HL - 1), :, pl.ds(0, 3 * part)], fwd_s.at[0])
    drained(ysend.at[pl.ds(0, HL - 1)], y_s.at[0])


def one_kernel(cores, token_devices, queries, keys, values, rates, fast_init, out_gain):
    blocks, rows, width = queries.shape
    HL, _, DH, _ = fast_init.shape
    G = token_devices // HL
    dma = lambda *shape: pltpu.SemaphoreType.DMA(shape)
    tokens = (2, HL, rows, DH)
    mats = (2, 3, DH, DH)
    any_space = pl.BlockSpec(memory_space=pl.ANY)
    in_vmem = pl.BlockSpec(memory_space=pltpu.VMEM)
    return pl.pallas_call(
        functools.partial(kernel, (cores, HL, G, rows, DH)),
        out_shape=(pltpu.VMEM(queries.shape, BF16), pltpu.VMEM(fast_init.shape, BF16)),
        in_specs=[any_space] * 6,
        out_specs=(in_vmem, in_vmem),
        scratch_shapes=[
            pltpu.VMEM((rows, width), BF16),
            pltpu.VMEM(fast_init.shape, BF16),
            pltpu.VMEM((HL,) + rates.shape, F32),
            pltpu.VMEM((1, width), F32),
            pltpu.VMEM((4, HL, rows, DH), BF16),
            pltpu.VMEM((HL, rows, DH), BF16),
            pltpu.VMEM(tokens, BF16),
            pltpu.VMEM(tokens, BF16),
            pltpu.VMEM(tokens, BF16),
            pltpu.VMEM(tokens, BF16),
            pltpu.VMEM(mats, F32),
            pltpu.VMEM(mats, BF16),
            pltpu.VMEM((2, 3, G - 1, DH // G, DH), BF16),
            pltpu.VMEM(mats, BF16),
            pltpu.VMEM((3, DH, DH), BF16),
            pltpu.VMEM((HL, rows, DH), BF16),
            pltpu.VMEM((HL, rows, DH), BF16),
            pltpu.VMEM((rows, width), F32),
            pltpu.VMEM((2, rows, 128), F32),
            pltpu.VMEM((2, cores - 1, rows, 128), F32),
            dma(9),
            dma(6), dma(2, HL - 1), dma(4),
            dma(2), dma(2, 3),
            dma(2), dma(2, 3, 3),
            dma(1), dma(3, HL - 1),
            dma(1), dma(2, 3, HL - 1),
            dma(1), dma(2), dma(2),
        ],
        compiler_params=pltpu.CompilerParams(collective_id=0, has_side_effects=True),
    )(queries, keys, values, rates, fast_init, out_gain.reshape(1, width))


def fits(cores, token_devices, queries, fast_init):
    blocks, rows, width = queries.shape
    HL, _, DH, _ = fast_init.shape
    return (
        blocks == 2 and HL > 1 and cores > 1 and token_devices == 4 * HL
        and rows == 128 and DH % 128 == 0
    )


def per_device_best(cores, token_devices, queries, keys, values, rates, fast_init, out_gain):
    if fits(cores, token_devices, queries, fast_init):
        return one_kernel(cores, token_devices, queries, keys, values, rates, fast_init, out_gain)
    return per_device(queries, keys, values, rates, fast_init, out_gain)


def solution(mesh):
    in_specs = (
        P(None, "tokens", "heads"),
        P(None, "tokens", "heads"),
        P(None, "tokens", "heads"),
        P(None, "heads", "tokens"),
        P("heads", None, None, None),
        P("heads"),
    )
    out_specs = (P(None, "tokens", "heads"), P("heads", None, None, None))
    return jax.shard_map(
        functools.partial(per_device_best, mesh.shape["heads"], mesh.shape["tokens"]), mesh=mesh, in_specs=in_specs, out_specs=out_specs, check_vma=False
    )
```
